32 devices in a mesh: lon: 4 (over y, core), lat: 8 (over z, x).
Axes of the slice: x: 2, y: 2, z: 4, core: 2. Of those that a mesh axis runs over, the one named last changes fastest.
Arguments:
- eta_adj: float32 [2048, 2048], P('lat', 'lon'), may hold values from -6 to 6
- east_adj: float32 [2048, 2048], P('lat', 'lon'), may hold values from -6 to 6
- north_adj: float32 [2048, 2048], P('lat', 'lon'), may hold values from -6 to 6
- depth: float32 [2048, 2048], P('lat', 'lon'), may hold values from 0.5 to 3
- station_owner: int32 [32768, 1], P(('lon', 'lat')), may hold values from 0 to 31; in each aligned block of 1024 rows (0 to 1023, 1024 to 2047, ...) at most 64 rows name the same one
- station_cell: int32 [32768], P(('lon', 'lat')), may hold values from 0 to 131071
- station_misfit: float32 [32768], P(('lon', 'lat')), may hold values from -6 to 6
- footprints: float32 [8192, 1024], P(('lon', 'lat')), may hold values from -0.1875 to 0.1875
- foot_tile: int32 [8192, 1], P(('lon', 'lat')), may hold values from 0 to 31; in each aligned block of 256 rows (0 to 255, 256 to 511, ...) at most 16 rows name the same one
- foot_block: int32 [8192], P(('lon', 'lat')), may hold values from 0 to 127
- foot_source: int32 [8192], P(('lon', 'lat')), may hold values from 0 to 19
Outputs:
- eta_start: float32 [2048, 2048], P('lat', 'lon')
- east_start: float32 [2048, 2048], P('lat', 'lon')
- north_start: float32 [2048, 2048], P('lat', 'lon')
- uplift_grad: float32 [4, 640], P(None, ('lon', 'lat'))
The draws below stay inside these ranges and needn't reach their ends.
Inputs may be any that keep to these rules, and one draw needn't show every extreme that they name: `station_owner`: in each device's 1024 rows (aligned blocks), no tile is named by more than 64 rows; some tile is named by exactly 64. `foot_tile`: in each device's 256 rows (aligned blocks), no tile is named by more than 16 rows; some tile is named by exactly 16.
All inputs are finite; a program needn't handle non-finite values.
Results may differ from the reference program's by a relative error of at most 0.0003.
Values sent between devices are 32-bit elements; how exact they have to be, the bound alone decides.
A program may use at most 64 MiB of HBM per device.

```python
import math
import jax
import jax.numpy as jnp
import numpy as np

CX = 512
CY = 256
ITERS = 4
STA_DEV = 256
FP_DEV = 256
SRC_DEV = 20
BH = 8
BW = 128
NX = 2048
NY = 2048
CELLS = 131072
NB = 128
SOURCES = 640
REC_DEV = 1024
RECORDS = 32768
FOOTS = 8192
CAP = 64
FCAP = 16
N_LON = 4
N_LAT = 8
DEVICES = 32


def plant(values, own_key, smallest, top_value):
    longest = values.shape.index(max(values.shape))
    spots = []
    for shift in (0, 1):
        where = [jax.random.randint(jax.random.fold_in(own_key, axis), (), 0, length) for axis, length in enumerate(values.shape)]
        where[longest] = (where[longest] + shift) % values.shape[longest]
        spots.append(tuple(where))
    return values.at[spots[0]].set(smallest).at[spots[1]].set(top_value)


def steps_of(rng, extent, shards, low, largest):
    gain, own = 1.0, jax.random.fold_in(rng, 6)
    for position, shards_of in shards:
        steps = jnp.exp(jax.random.uniform(jax.random.fold_in(own, position), (shards_of,), jnp.float32, low / len(shards), largest / len(shards)))
        gain = gain * jnp.repeat(steps, extent[position] // shards_of).reshape([-1 if axis == position else 1 for axis in range(len(extent))])
    return gain


def assign_block(rng, own, number, rows, amount, top, bound, skew):
    ranking = jax.random.permutation(rng, amount)
    heavy_load, usual = load_shares(amount, rows * top, bound, skew, True), load_shares(amount, rows * top, bound, skew, False)
    places = jnp.arange(amount)

    def named(lengths, offset_by):
        used = int((lengths > 0).sum())
        fixed = max(1, used // 4)
        moved = fixed + (places - fixed + offset_by * (used - fixed)) % max(1, amount - fixed)
        return jnp.zeros((amount,), jnp.int32).at[ranking[jnp.where(places < fixed, places, moved)]].set(jnp.asarray(lengths, jnp.int32))

    lengths = jnp.where(number % 4 == 0, named(heavy_load, number // 4), named(usual, number - number // 4 - 1))
    mixed = jax.random.permutation(jax.random.fold_in(own, 3), amount)
    giver, taker = mixed[0:amount // 2 * 2:2], mixed[1:amount // 2 * 2:2]
    margin = jnp.minimum(lengths[giver] - 1, bound - lengths[taker]) // 2
    margin = jnp.where((giver == ranking[0]) | (taker == ranking[0]) | (lengths[taker] == 0), 0, jnp.maximum(margin, 0))
    moved = jax.random.randint(jax.random.fold_in(own, 4), (amount // 2,), 0, 1 << 20) % (margin + 1)
    lengths = lengths.at[giver].add(-moved).at[taker].add(moved)
    members = jnp.searchsorted(jnp.cumsum(lengths), jnp.arange(rows * top), side="right").astype(jnp.int32)
    grid = members.reshape(top, rows).T
    grid = grid[jax.random.permutation(jax.random.fold_in(own, 1), rows)]
    offset_by = jax.random.randint(jax.random.fold_in(own, 2), (rows, 1), 0, top)
    return jnp.take_along_axis(grid, (jnp.arange(top)[None, :] + offset_by) % top, axis=1)


def load_shares(amount, total, limit, slope, full):
    loads = [(1 << 20) // math.isqrt(standing ** slope) + 1 for standing in range(1, amount + 1)]
    largest = limit if full else min(limit, max(-(-total // amount), total * loads[0] // sum(loads)))
    least = 1 if total - largest >= amount - 1 else 0
    holding, rest = [largest] + [least] * (amount - 1), total - largest - least * (amount - 1)
    while rest > 0:
        candidates = [i for i in range(1, amount) if holding[i] < largest] or [i for i in range(1, amount) if holding[i] < limit]
        whole, remaining = sum([loads[i] for i in candidates]), rest
        for i in candidates:
            more = min(limit - holding[i], max(1, remaining * loads[i] // whole), rest)
            holding[i] = holding[i] + more
            rest = rest - more
    return np.array(holding)


def normal_values(own_key, dims, scale, reach, shards=(), held_as=jnp.bfloat16):
    entries = jax.random.normal(own_key, dims, jnp.float32) * scale
    if len(shards) > 0:
        entries = steps_of(own_key, dims, shards, -0.22, 0.18) * entries
    return jnp.clip(entries, min=-reach, max=reach).astype(held_as)


def setup_inputs(seed: int = 0) -> dict:
    key_list = jax.random.split(jax.random.key(seed), 12)
    eta_adj = normal_values(key_list[0], (NY, NX), 1.0, 6.0, ((0, 8), (1, 4)), jnp.float32)
    east_adj = normal_values(key_list[1], (NY, NX), 1.0, 6.0, ((0, 8), (1, 4)), jnp.float32)
    north_adj = normal_values(key_list[2], (NY, NX), 1.0, 6.0, ((0, 8), (1, 4)), jnp.float32)
    depth = jnp.clip(jnp.exp(math.log(3.0) - 1.7917595 * jax.random.uniform(key_list[3], (NY, NX), jnp.float32) ** steps_of(key_list[3], (NY, NX), ((0, 8), (1, 4)), -0.2, 0.2)), 0.5, 3.0)
    station_owner_keys = jax.random.split(jax.random.fold_in(key_list[4], 1), RECORDS // REC_DEV)
    station_owner_turns = jax.random.permutation(jax.random.fold_in(key_list[4], 3), RECORDS // REC_DEV)
    station_owner = jax.vmap(lambda own, number: assign_block(jax.random.fold_in(key_list[4], 2), own, number, REC_DEV, DEVICES, 1, CAP, 2))(station_owner_keys, station_owner_turns).reshape((RECORDS, 1))
    station_cell = plant(jax.random.randint(key_list[5], (RECORDS,), 0, CELLS), jax.random.fold_in(key_list[5], 1), 0, CELLS - 1).astype(jnp.int32)
    station_misfit = normal_values(key_list[6], (RECORDS,), 1.0, 6.0, ((0, 32),), jnp.float32)
    footprints = normal_values(key_list[7], (FOOTS, BH * BW), (BH * BW) ** -0.5, 0.1875, ((0, 32),), jnp.float32)
    foot_tile_keys = jax.random.split(jax.random.fold_in(key_list[8], 1), FOOTS // FP_DEV)
    foot_tile_turns = jax.random.permutation(jax.random.fold_in(key_list[8], 3), FOOTS // FP_DEV)
    foot_tile = jax.vmap(lambda own, number: assign_block(jax.random.fold_in(key_list[8], 2), own, number, FP_DEV, DEVICES, 1, FCAP, 1))(foot_tile_keys, foot_tile_turns).reshape((FOOTS, 1))
    foot_block = plant(jax.random.randint(key_list[9], (FOOTS,), 0, NB), jax.random.fold_in(key_list[9], 1), 0, NB - 1).astype(jnp.int32)
    foot_source = plant(jax.random.randint(key_list[10], (FOOTS,), 0, SRC_DEV), jax.random.fold_in(key_list[10], 1), 0, SRC_DEV - 1).astype(jnp.int32)
    return {"eta_adj": eta_adj, "east_adj": east_adj, "north_adj": north_adj, "depth": depth, "station_owner": station_owner, "station_cell": station_cell, "station_misfit": station_misfit, "footprints": footprints, "foot_tile": foot_tile, "foot_block": foot_block, "foot_source": foot_source}


GRAVITY_STEP = 0.8
DEPTH_STEP = 0.8
TURN_RATE = 0.1
RETAIN = 0.97


def east_diff(padded):
    return 0.5 * (padded[..., 1:-1, 2:] - padded[..., 1:-1, :-2])


def north_diff(padded):
    return 0.5 * (padded[..., 2:, 1:-1] - padded[..., :-2, 1:-1])


def with_border(field):
    widths = [(0, 0)] * (field.ndim - 2) + [(1, 1), (1, 1)]
    return jnp.pad(field, widths)


def reference(eta_adj, east_adj, north_adj, depth, station_owner, station_cell, station_misfit, footprints, foot_tile, foot_block, foot_source):
    record_rows = jnp.arange(RECORDS, dtype=jnp.int32)
    period_of = (record_rows % REC_DEV) // STA_DEV
    owner = station_owner[:, 0]
    lat_of = (owner % N_LAT) * CY + station_cell // CX
    lon_of = (owner // N_LAT) * CX + station_cell % CX
    forcing = jnp.zeros((ITERS, NY, NX), jnp.float32).at[period_of, lat_of, lon_of].add(station_misfit)
    tiles = foot_tile[:, 0]
    tile_lat = tiles % N_LAT
    tile_lon = tiles // N_LAT
    block_row = foot_block // (CX // BW)
    block_col = foot_block % (CX // BW)
    global_source = (jnp.arange(FOOTS, dtype=jnp.int32) // FP_DEV) * SRC_DEV + foot_source
    height, east, north = eta_adj, east_adj, north_adj
    grads = [None] * ITERS
    for period in range(ITERS - 1, -1, -1):
        flows = with_border(jnp.stack([east, north]))
        pressure = height + forcing[period] - GRAVITY_STEP * (east_diff(flows[0]) + north_diff(flows[1]))
        flux = with_border(depth * pressure)
        east_new = RETAIN * east + TURN_RATE * north - DEPTH_STEP * east_diff(flux)
        north_new = RETAIN * north - TURN_RATE * east - DEPTH_STEP * north_diff(flux)
        height, east, north = pressure, east_new, north_new
        tiled = height.reshape(N_LAT, CY // BH, BH, N_LON, CX // BW, BW)
        blocks = tiled[tile_lat, block_row, :, tile_lon, block_col, :].reshape(FOOTS, BH * BW)
        partial_value = jnp.sum(blocks * footprints, axis=1)
        grads[period] = jax.ops.segment_sum(partial_value, global_source, num_segments=SOURCES)
    return height, east, north, jnp.stack(grads)
```

```python
import functools

import jax
import jax.numpy as jnp
from jax import lax
from jax.experimental import pallas as pl
from jax.experimental.pallas import tpu as pltpu
from jax.sharding import PartitionSpec as P

ITERS = 4
STA_DEV = 256
SRC_DEV = 20
BH = 8
BW = 128
EDGE = 2 * ITERS
LANES = 128
FIELDS = 4 + ITERS

GRAVITY_STEP = 0.8
DEPTH_STEP = 0.8
TURN_RATE = 0.1
RETAIN = 0.97

MESH = pl.DeviceIdType.MESH
F32 = jnp.float32
BF16 = jnp.bfloat16


def split(values):
    high = values.astype(BF16)
    return high, (values - high.astype(F32)).astype(BF16)


def rolled(values, shift, axis):
    return pltpu.roll(values, shift % values.shape[axis], axis)


def central(values, axis):
    return rolled(values, -1, axis) - rolled(values, 1, axis)


def nt_dot(left, right):
    return lax.dot_general(left, right, (((1,), (1,)), ((), ())), preferred_element_type=F32)


def kernel(
    lon_count,
    lat_count,
    limit,
    eta_ref,
    east_ref,
    north_ref,
    depth_ref,
    packet_ref,
    feet_ref,
    eta_out,
    east_out,
    north_out,
    back_out,
    arrived,
    held,
    ext,
    to_east,
    to_west,
    from_west,
    from_east,
    blocks,
    partial,
    sta_send,
    sta_recv,
    foot_send,
    foot_recv,
    back_send,
    back_recv,
    edge_send,
    edge_recv,
):
    lon = lax.axis_index("lon")
    lat = lax.axis_index("lat")
    devices = lon_count * lat_count
    me = lon * lat_count + lat
    rows, cols = eta_ref.shape
    tail = cols
    wide = cols + LANES
    tall = rows + 2 * EDGE
    slots = devices * limit
    group = partial.shape[0]
    per_group = devices // group

    def peer(i):
        return lax.rem(me + i, devices)

    def place(d):
        return (d // lat_count, lax.rem(d, lat_count))

    barrier = pltpu.get_barrier_semaphore()

    @pl.loop(1, devices)
    def _(i):
        pl.semaphore_signal(barrier, inc=1, device_id=place(peer(i)), device_id_type=MESH)

    pl.semaphore_wait(barrier, devices - 1)

    def sta_copy(to, slot):
        return pltpu.make_async_remote_copy(
            src_ref=packet_ref.at[to],
            dst_ref=arrived.at[slot],
            send_sem=sta_send.at[to],
            recv_sem=sta_recv.at[slot],
            device_id=place(to),
            device_id_type=MESH,
        )

    def foot_copy(to, slot):
        return pltpu.make_async_remote_copy(
            src_ref=feet_ref.at[pl.ds(pl.multiple_of(to * limit, 8), limit)],
            dst_ref=held.at[pl.ds(pl.multiple_of(slot * limit, 8), limit)],
            send_sem=foot_send.at[to],
            recv_sem=foot_recv.at[slot],
            device_id=place(to),
            device_id_type=MESH,
        )

    def back_copy(to, slot):
        return pltpu.make_async_remote_copy(
            src_ref=partial.at[to // per_group],
            dst_ref=back_out.at[slot],
            send_sem=back_send.at[to],
            recv_sem=back_recv.at[slot],
            device_id=place(to),
            device_id_type=MESH,
        )

    def start_feet(low, high):
        @pl.loop(low, high)
        def _(i):
            foot_copy(peer(i), me).start()

    @pl.loop(1, devices)
    def _(i):
        sta_copy(peer(i), me).start()

    first = 1 + devices // 4
    second = first + devices // 8
    start_feet(1, first)

    arrived[me] = packet_ref[me]
    own = pl.ds(pl.multiple_of(me * limit, 8), limit)
    held[own] = feet_ref[own]
    for field, ref in enumerate((eta_ref, east_ref, north_ref, depth_ref)):
        ext[field, :rows, :cols] = ref[...]
    for k in range(ITERS):
        ext[4 + k, :rows, :cols] = jnp.zeros((rows, cols), F32)

    @pl.loop(1, devices)
    def _(i):
        sta_copy(me, peer(i)).wait_recv()

    width = packet_ref.shape[2]
    bunch = 4
    high_lane = lax.rem(lax.broadcasted_iota(jnp.int32, (1, bunch * width), 1), width) < width // 2
    row_id = lax.broadcasted_iota(jnp.int32, (rows, bunch * width), 0).astype(F32)
    col_id = lax.broadcasted_iota(jnp.int32, (cols, bunch * width), 0).astype(F32)

    @pl.loop(0, devices // bunch)
    def _(g):
        def line(q):
            return jnp.concatenate(
                [arrived[g * bunch + j, q : q + 1, :] for j in range(bunch)], axis=1
            )

        amount, at_row, at_col = line(0), line(1), line(2)
        high = amount.astype(BF16).astype(F32)
        piece = jnp.where(high_lane, high, amount - high)
        right = jnp.where(col_id == at_col, piece, 0.0).astype(BF16)
        for k in range(ITERS):
            left = jnp.where(row_id == at_row - k * rows, 1.0, 0.0).astype(BF16)
            ext[4 + k, :rows, :cols] += nt_dot(left, right)

    lane = lax.broadcasted_iota(jnp.int32, (rows, LANES), 1)

    def strip(low, start):
        out = jnp.zeros((rows, LANES), F32)
        for field in range(FIELDS):
            tile = ext[field, :rows, low : low + LANES]
            moved = rolled(tile, EDGE * field - start, 1)
            inside = (lane >= EDGE * field) & (lane < EDGE * (field + 1))
            out = jnp.where(inside, moved, out)
        return out

    to_east[...] = strip(cols - LANES, LANES - EDGE)
    to_west[...] = strip(0, 0)

    def edge_copy(src, dst, number, to):
        return pltpu.make_async_remote_copy(
            src_ref=src,
            dst_ref=dst,
            send_sem=edge_send.at[number],
            recv_sem=edge_recv.at[number],
            device_id=to,
            device_id_type=MESH,
        )

    has_west, has_east = lon > 0, lon < lon_count - 1
    has_north, has_south = lat > 0, lat < lat_count - 1
    east_copy = edge_copy(to_east, from_west, 0, (lax.rem(lon + 1, lon_count), lat))
    west_copy = edge_copy(to_west, from_east, 1, (lax.rem(lon + lon_count - 1, lon_count), lat))
    south_copy = edge_copy(
        ext.at[:, rows - EDGE : rows, :],
        ext.at[:, rows + EDGE : tall, :],
        2,
        (lon, lax.rem(lat + 1, lat_count)),
    )
    north_copy = edge_copy(
        ext.at[:, 0:EDGE, :],
        ext.at[:, rows : rows + EDGE, :],
        3,
        (lon, lax.rem(lat + lat_count - 1, lat_count)),
    )

    pl.when(has_east)(east_copy.start)
    pl.when(has_west)(west_copy.start)
    start_feet(first, second)

    @pl.when(lon == 0)
    def _():
        from_west[...] = jnp.zeros((rows, LANES), F32)

    @pl.when(lon == lon_count - 1)
    def _():
        from_east[...] = jnp.zeros((rows, LANES), F32)

    pl.when(has_west)(east_copy.wait_recv)
    pl.when(has_east)(west_copy.wait_recv)
    for field in range(FIELDS):
        after = rolled(from_east[...], -EDGE * field, 1)
        before = rolled(from_west[...], LANES - EDGE - EDGE * field, 1)
        ext[field, :rows, tail:] = jnp.where(
            lane < EDGE, after, jnp.where(lane >= LANES - EDGE, before, 0.0)
        )

    pl.when(has_south)(south_copy.start)
    pl.when(has_north)(north_copy.start)
    start_feet(second, devices)

    @pl.when(lat == 0)
    def _():
        ext[:, rows + EDGE : tall, :] = jnp.zeros((FIELDS, EDGE, wide), F32)

    @pl.when(lat == lat_count - 1)
    def _():
        ext[:, rows : rows + EDGE, :] = jnp.zeros((FIELDS, EDGE, wide), F32)

    pl.when(has_north)(south_copy.wait_recv)
    pl.when(has_south)(north_copy.wait_recv)
    pl.when(has_east)(east_copy.wait_send)
    pl.when(has_west)(west_copy.wait_send)
    pl.when(has_south)(south_copy.wait_send)
    pl.when(has_north)(north_copy.wait_send)

    at_row = lax.broadcasted_iota(jnp.int32, (tall, wide), 0)
    at_col = lax.broadcasted_iota(jnp.int32, (tall, wide), 1)
    row_end = rows + jnp.where(has_south, EDGE, 0)
    row_begin = tall - jnp.where(has_north, EDGE, 0)
    col_end = cols + jnp.where(has_east, EDGE, 0)
    col_begin = wide - jnp.where(has_west, EDGE, 0)
    inside = ((at_row < row_end) | (at_row >= row_begin)) & (
        (at_col < col_end) | (at_col >= col_begin)
    )
    mask = jnp.where(inside, 1.0, 0.0)

    bands = rows // BH
    block_cols = cols // BW
    count = bands * block_cols
    for period in range(ITERS - 1, -1, -1):
        east, north = ext[1], ext[2]
        pressure = (
            ext[0] + ext[4 + period] - 0.5 * GRAVITY_STEP * (central(east, 1) + central(north, 0))
        )
        ext[0] = pressure
        flux = ext[3] * pressure
        ext[1] = mask * (
            RETAIN * east + TURN_RATE * north - 0.5 * DEPTH_STEP * central(flux, 1)
        )
        ext[2] = mask * (
            RETAIN * north - TURN_RATE * east - 0.5 * DEPTH_STEP * central(flux, 0)
        )
        for c in range(block_cols):
            tiles = ext[0, :rows, c * BW : (c + 1) * BW].reshape(bands, BH, BW)
            for r in range(BH):
                low = period * count + c * bands
                blocks[low : low + bands, r * BW : (r + 1) * BW] = tiles[:, r, :]

    eta_out[...] = ext[0, :rows, :cols]
    east_out[...] = ext[1, :rows, :cols]
    north_out[...] = ext[2, :rows, :cols]

    ids = jnp.sum(arrived[:, 4 : 4 + group, :], axis=0)
    block_high, block_low = split(blocks[...])
    number = lax.broadcasted_iota(jnp.int32, (count, LANES), 0)
    number = (lax.rem(number, bands) * block_cols + number // bands).astype(F32)

    @pl.loop(1, devices)
    def _(i):
        foot_copy(me, peer(i)).wait_recv()

    for g in range(group):
        foot_high, foot_low = split(held[g * LANES : (g + 1) * LANES, :])
        both = (
            nt_dot(block_high, foot_high)
            + nt_dot(block_high, foot_low)
            + nt_dot(block_low, foot_high)
        )
        wanted = number == ids[g : g + 1, :]
        for k in range(ITERS):
            found = jnp.where(wanted, both[k * count : (k + 1) * count], 0.0)
            partial[g, k : k + 1, :] = jnp.sum(found, axis=0, keepdims=True)
        partial[g, ITERS:, :] = jnp.zeros((8 - ITERS, LANES), F32)

    @pl.loop(1, devices)
    def _(i):
        back_copy(peer(i), me).start()

    back_out[me] = partial[me // per_group]

    @pl.loop(1, devices)
    def _(i):
        sta_copy(peer(i), me).wait_send()
        foot_copy(peer(i), me).wait_send()
        back_copy(peer(i), me).wait_send()
        back_copy(me, peer(i)).wait_recv()


def ranks(one_hot):
    size = one_hot.shape[0]
    at = jnp.arange(size, dtype=jnp.int32)
    lower = (at[:, None] > at[None, :]).astype(BF16)
    before = jnp.dot(lower, one_hot.astype(BF16), preferred_element_type=F32)
    return jnp.sum(before * one_hot, axis=1)


def exact_dot(left, right):
    return jnp.dot(left, right, precision=lax.Precision.HIGHEST, preferred_element_type=F32)


def shards(
    lon_count,
    lat_count,
    eta_adj,
    east_adj,
    north_adj,
    depth,
    station_owner,
    station_cell,
    station_misfit,
    footprints,
    foot_tile,
    foot_block,
    foot_source,
):
    devices = lon_count * lat_count
    rows, cols = eta_adj.shape
    records = station_cell.shape[0]
    feet = footprints.shape[0]
    capacity = max(2, 2 * records // devices)
    width = max(LANES, 2 * capacity)
    limit = max(8, 2 * feet // devices)
    slots = devices * limit
    group = slots // LANES
    me = lax.axis_index("lon") * lat_count + lax.axis_index("lat")
    names = jnp.arange(devices, dtype=jnp.int32)

    owner_hot = (station_owner == names[None, :]).astype(F32)
    rank = ranks(owner_hot)
    lanes = (jnp.arange(width, dtype=jnp.int32) % (width // 2)).astype(F32)
    slot_hot = (rank[:, None] == lanes[None, :]).astype(F32)
    period = jnp.arange(records, dtype=jnp.int32) // STA_DEV
    at_row = (period * rows + station_cell // cols).astype(F32)
    at_col = (station_cell % cols).astype(F32)
    spread = jnp.concatenate(
        [slot_hot * v[:, None] for v in (station_misfit, at_row, at_col)], axis=1
    )
    stations = exact_dot(owner_hot.T, spread).reshape(devices, 3, width)

    tile_hot = (foot_tile == names[None, :]).astype(F32)
    foot_place = foot_tile[:, 0] * limit + ranks(tile_hot).astype(jnp.int32)
    place_hot = (jnp.arange(slots, dtype=jnp.int32)[:, None] == foot_place[None, :]).astype(F32)
    foot_buffer = exact_dot(place_hot, footprints)
    ids = jnp.sum(place_hot * foot_block.astype(F32)[None, :], axis=1).reshape(devices, 1, limit)
    mine = (names == me).astype(F32)
    ids = (ids * mine[None, :, None]).reshape(devices, group, LANES)
    if width > LANES:
        ids = jnp.pad(ids, ((0, 0), (0, 0), (0, width - LANES)))
    packet = jnp.concatenate([stations, jnp.zeros((devices, 1, width), F32), ids], axis=1)
    depth_of = packet.shape[1]
    packet = jnp.pad(packet, ((0, 0), (0, -depth_of % 8), (0, 0)))
    depth_of = packet.shape[1]

    source_hot = (foot_source[:, None] == jnp.arange(SRC_DEV, dtype=jnp.int32)[None, :]).astype(F32)
    source_of = exact_dot(place_hot, source_hot)

    tall, wide = rows + 2 * EDGE, cols + LANES
    count = (rows // BH) * (cols // BW)
    vmem = pl.BlockSpec(memory_space=pltpu.VMEM)
    field = jax.ShapeDtypeStruct((rows, cols), F32)
    eta, east, north, back = pl.pallas_call(
        functools.partial(kernel, lon_count, lat_count, limit),
        out_shape=(field, field, field, jax.ShapeDtypeStruct((devices, 8, LANES), F32)),
        in_specs=[vmem] * 6,
        out_specs=(vmem,) * 4,
        scratch_shapes=[
            pltpu.VMEM((devices, depth_of, width), F32),
            pltpu.VMEM((slots, BH * BW), F32),
            pltpu.VMEM((FIELDS, tall, wide), F32),
            pltpu.VMEM((rows, LANES), F32),
            pltpu.VMEM((rows, LANES), F32),
            pltpu.VMEM((rows, LANES), F32),
            pltpu.VMEM((rows, LANES), F32),
            pltpu.VMEM((ITERS * count, BH * BW), F32),
            pltpu.VMEM((group, 8, LANES), F32),
            pltpu.SemaphoreType.DMA((devices,)),
            pltpu.SemaphoreType.DMA((devices,)),
            pltpu.SemaphoreType.DMA((devices,)),
            pltpu.SemaphoreType.DMA((devices,)),
            pltpu.SemaphoreType.DMA((devices,)),
            pltpu.SemaphoreType.DMA((devices,)),
            pltpu.SemaphoreType.DMA((4,)),
            pltpu.SemaphoreType.DMA((4,)),
        ],
        compiler_params=pltpu.CompilerParams(
            collective_id=0, has_side_effects=True, vmem_limit_bytes=60 * 1024 * 1024
        ),
    )(eta_adj, east_adj, north_adj, depth, packet, foot_buffer)

    start = lax.rem(me, devices // group) * limit
    mine_back = lax.dynamic_slice(back, (0, 0, start), (devices, ITERS, limit))
    by_slot = mine_back.transpose(1, 0, 2).reshape(ITERS, slots)
    uplift_grad = exact_dot(by_slot, source_of)
    return eta, east, north, uplift_grad


def solution(mesh):
    in_specs = (
        P("lat", "lon"),
        P("lat", "lon"),
        P("lat", "lon"),
        P("lat", "lon"),
        P(("lon", "lat"), None),
        P(("lon", "lat")),
        P(("lon", "lat")),
        P(("lon", "lat"), None),
        P(("lon", "lat"), None),
        P(("lon", "lat")),
        P(("lon", "lat")),
    )
    out_specs = (P("lat", "lon"), P("lat", "lon"), P("lat", "lon"), P(None, ("lon", "lat")))
    body = functools.partial(shards, mesh.shape["lon"], mesh.shape["lat"])
    return jax.shard_map(body, mesh=mesh, in_specs=in_specs, out_specs=out_specs, check_vma=False)
```

```python
import functools

import jax
import jax.numpy as jnp
from jax import lax
from jax.experimental import pallas as pl
from jax.experimental.pallas import tpu as pltpu
from jax.sharding import PartitionSpec as P

ITERS = 4
STA_DEV = 256
SRC_DEV = 20
BH = 8
BW = 128
EDGE = 2 * ITERS
LANES = 128
FIELDS = 4 + ITERS

GRAVITY_STEP = 0.8
DEPTH_STEP = 0.8
TURN_RATE = 0.1
RETAIN = 0.97

MESH = pl.DeviceIdType.MESH
F32 = jnp.float32
BF16 = jnp.bfloat16


def split(values):
    high = values.astype(BF16)
    return high, (values - high.astype(F32)).astype(BF16)


def rolled(values, shift, axis):
    return pltpu.roll(values, shift % values.shape[axis], axis)


def central(values, axis):
    return rolled(values, -1, axis) - rolled(values, 1, axis)


def nt_dot(left, right):
    return lax.dot_general(left, right, (((1,), (1,)), ((), ())), preferred_element_type=F32)


def kernel(
    lon_count,
    lat_count,
    limit,
    eta_ref,
    east_ref,
    north_ref,
    depth_ref,
    packet_ref,
    feet_ref,
    eta_out,
    east_out,
    north_out,
    back_out,
    arrived,
    held,
    ext,
    to_east,
    to_west,
    from_west,
    from_east,
    blocks,
    partial,
    ids_ref,
    sta_send,
    sta_recv,
    foot_send,
    foot_recv,
    back_send,
    back_recv,
    edge_send,
    edge_recv,
):
    lon = lax.axis_index("lon")
    lat = lax.axis_index("lat")
    devices = lon_count * lat_count
    me = lon * lat_count + lat
    rows, cols = eta_ref.shape
    tail = cols
    wide = cols + LANES
    tall = rows + 2 * EDGE
    slots = devices * limit
    group = partial.shape[0]
    per_group = devices // group

    def peer(i):
        return lax.rem(me + i, devices)

    def spread_peer(i):
        turn = lax.rem(i, lat_count)
        turn = lax.rem(turn, 2) * (lat_count // 2) + turn // 2
        return lax.rem(lon + i // lat_count, lon_count) * lat_count + lax.rem(
            lat + turn, lat_count
        )

    def place(d):
        return (d // lat_count, lax.rem(d, lat_count))

    barrier = pltpu.get_barrier_semaphore()

    @pl.loop(1, devices)
    def _(i):
        pl.semaphore_signal(barrier, inc=1, device_id=place(peer(i)), device_id_type=MESH)

    pl.semaphore_wait(barrier, devices - 1)

    def sta_copy(to, slot):
        return pltpu.make_async_remote_copy(
            src_ref=packet_ref.at[to],
            dst_ref=arrived.at[slot],
            send_sem=sta_send.at[to],
            recv_sem=sta_recv.at[slot],
            device_id=place(to),
            device_id_type=MESH,
        )

    def foot_copy(to, slot):
        return pltpu.make_async_remote_copy(
            src_ref=feet_ref.at[pl.ds(pl.multiple_of(to * limit, 8), limit)],
            dst_ref=held.at[pl.ds(pl.multiple_of(slot * limit, 8), limit)],
            send_sem=foot_send.at[to],
            recv_sem=foot_recv.at[slot],
            device_id=place(to),
            device_id_type=MESH,
        )

    def back_copy(to, slot):
        return pltpu.make_async_remote_copy(
            src_ref=partial.at[to // per_group],
            dst_ref=back_out.at[slot],
            send_sem=back_send.at[to],
            recv_sem=back_recv.at[slot],
            device_id=place(to),
            device_id_type=MESH,
        )

    def start_feet(low, high):
        @pl.loop(low, high)
        def _(i):
            foot_copy(spread_peer(i), me).start()

    @pl.loop(1, devices)
    def _(i):
        sta_copy(peer(i), me).start()

    first = 1 + 3 * devices // 8
    second = first + devices // 8
    start_feet(1, first)

    arrived[me] = packet_ref[me]
    own = pl.ds(pl.multiple_of(me * limit, 8), limit)
    held[own] = feet_ref[own]
    for field, ref in enumerate((eta_ref, east_ref, north_ref, depth_ref)):
        ext[field, :rows, :cols] = ref[...]
    for k in range(ITERS):
        ext[4 + k, :rows, :cols] = jnp.zeros((rows, cols), F32)

    @pl.loop(1, devices)
    def _(i):
        sta_copy(me, peer(i)).wait_recv()

    width = packet_ref.shape[2]
    bunch = 4
    high_lane = lax.rem(lax.broadcasted_iota(jnp.int32, (1, bunch * width), 1), width) < width // 2
    row_id = lax.broadcasted_iota(jnp.int32, (rows, bunch * width), 0).astype(F32)
    col_id = lax.broadcasted_iota(jnp.int32, (cols, bunch * width), 0).astype(F32)

    @pl.loop(0, devices // bunch)
    def _(g):
        def line(q):
            return jnp.concatenate(
                [arrived[g * bunch + j, q : q + 1, :] for j in range(bunch)], axis=1
            )

        amount, at_row, at_col = line(0), line(1), line(2)
        high = amount.astype(BF16).astype(F32)
        piece = jnp.where(high_lane, high, amount - high)
        right = jnp.where(col_id == at_col, piece, 0.0).astype(BF16)
        for k in range(ITERS):
            left = jnp.where(row_id == at_row - k * rows, 1.0, 0.0).astype(BF16)
            ext[4 + k, :rows, :cols] += nt_dot(left, right)

    lane = lax.broadcasted_iota(jnp.int32, (rows, LANES), 1)

    def strip(low, start):
        out = jnp.zeros((rows, LANES), F32)
        for field in range(FIELDS):
            tile = ext[field, :rows, low : low + LANES]
            moved = rolled(tile, EDGE * field - start, 1)
            inside = (lane >= EDGE * field) & (lane < EDGE * (field + 1))
            out = jnp.where(inside, moved, out)
        return out

    to_east[...] = strip(cols - LANES, LANES - EDGE)
    to_west[...] = strip(0, 0)

    def edge_copy(src, dst, number, to):
        return pltpu.make_async_remote_copy(
            src_ref=src,
            dst_ref=dst,
            send_sem=edge_send.at[number],
            recv_sem=edge_recv.at[number],
            device_id=to,
            device_id_type=MESH,
        )

    has_west, has_east = lon > 0, lon < lon_count - 1
    has_north, has_south = lat > 0, lat < lat_count - 1
    east_copy = edge_copy(to_east, from_west, 0, (lax.rem(lon + 1, lon_count), lat))
    west_copy = edge_copy(to_west, from_east, 1, (lax.rem(lon + lon_count - 1, lon_count), lat))
    south_copy = edge_copy(
        ext.at[:, rows - EDGE : rows, :],
        ext.at[:, rows + EDGE : tall, :],
        2,
        (lon, lax.rem(lat + 1, lat_count)),
    )
    north_copy = edge_copy(
        ext.at[:, 0:EDGE, :],
        ext.at[:, rows : rows + EDGE, :],
        3,
        (lon, lax.rem(lat + lat_count - 1, lat_count)),
    )

    pl.when(has_east)(east_copy.start)
    pl.when(has_west)(west_copy.start)
    start_feet(first, second)

    @pl.when(lon == 0)
    def _():
        from_west[...] = jnp.zeros((rows, LANES), F32)

    @pl.when(lon == lon_count - 1)
    def _():
        from_east[...] = jnp.zeros((rows, LANES), F32)

    pl.when(has_west)(east_copy.wait_recv)
    pl.when(has_east)(west_copy.wait_recv)
    for field in range(FIELDS):
        after = rolled(from_east[...], -EDGE * field, 1)
        before = rolled(from_west[...], LANES - EDGE - EDGE * field, 1)
        ext[field, :rows, tail:] = jnp.where(
            lane < EDGE, after, jnp.where(lane >= LANES - EDGE, before, 0.0)
        )

    pl.when(has_south)(south_copy.start)
    pl.when(has_north)(north_copy.start)
    start_feet(second, devices)

    @pl.when(lat == 0)
    def _():
        ext[:, rows + EDGE : tall, :] = jnp.zeros((FIELDS, EDGE, wide), F32)

    @pl.when(lat == lat_count - 1)
    def _():
        ext[:, rows : rows + EDGE, :] = jnp.zeros((FIELDS, EDGE, wide), F32)

    pl.when(has_north)(south_copy.wait_recv)
    pl.when(has_south)(north_copy.wait_recv)
    pl.when(has_east)(east_copy.wait_send)
    pl.when(has_west)(west_copy.wait_send)
    pl.when(has_south)(south_copy.wait_send)
    pl.when(has_north)(north_copy.wait_send)

    at_row = lax.broadcasted_iota(jnp.int32, (tall, wide), 0)
    at_col = lax.broadcasted_iota(jnp.int32, (tall, wide), 1)
    row_end = rows + jnp.where(has_south, EDGE, 0)
    row_begin = tall - jnp.where(has_north, EDGE, 0)
    col_end = cols + jnp.where(has_east, EDGE, 0)
    col_begin = wide - jnp.where(has_west, EDGE, 0)
    inside = ((at_row < row_end) | (at_row >= row_begin)) & (
        (at_col < col_end) | (at_col >= col_begin)
    )
    mask = jnp.where(inside, 1.0, 0.0)

    bands = rows // BH
    block_cols = cols // BW
    count = bands * block_cols
    for period in range(ITERS - 1, -1, -1):
        east, north = ext[1], ext[2]
        pressure = (
            ext[0] + ext[4 + period] - 0.5 * GRAVITY_STEP * (central(east, 1) + central(north, 0))
        )
        ext[0] = pressure
        flux = ext[3] * pressure
        ext[1] = mask * (
            RETAIN * east + TURN_RATE * north - 0.5 * DEPTH_STEP * central(flux, 1)
        )
        ext[2] = mask * (
            RETAIN * north - TURN_RATE * east - 0.5 * DEPTH_STEP * central(flux, 0)
        )
        for c in range(block_cols):
            tiles = ext[0, :rows, c * BW : (c + 1) * BW].reshape(bands, BH, BW)
            for r in range(BH):
                low = period * count + c * bands
                blocks[low : low + bands, r * BW : (r + 1) * BW] = tiles[:, r, :]

    eta_out[...] = ext[0, :rows, :cols]
    east_out[...] = ext[1, :rows, :cols]
    north_out[...] = ext[2, :rows, :cols]

    ids = jnp.sum(arrived[:, 4 : 4 + group, :], axis=0)
    block_high, block_low = split(blocks[...])
    number = lax.broadcasted_iota(jnp.int32, (count, LANES), 0)
    number = (lax.rem(number, bands) * block_cols + number // bands).astype(F32)

    for g in range(group):
        ids_ref[g] = jnp.broadcast_to(ids[g : g + 1, :], (8, LANES))
        partial[g] = jnp.zeros((8, LANES), F32)
    mine = me // per_group

    @pl.loop(0, group)
    def _(j):
        g = lax.rem(mine + group - j, group)

        @pl.loop(0, per_group)
        def _(t):
            source = g * per_group + t
            pl.when(source != me)(foot_copy(me, source).wait_recv)

        foot_high, foot_low = split(held[pl.ds(pl.multiple_of(g * LANES, LANES), LANES), :])
        both = (
            nt_dot(block_high, foot_high)
            + nt_dot(block_high, foot_low)
            + nt_dot(block_low, foot_high)
        )
        wanted = number == ids_ref[g][:1]
        for k in range(ITERS):
            found = jnp.where(wanted, both[k * count : (k + 1) * count], 0.0)
            partial[g, k : k + 1, :] = jnp.sum(found, axis=0, keepdims=True)

        @pl.loop(0, per_group)
        def _(t):
            owner = g * per_group + t
            pl.when(owner != me)(back_copy(owner, me).start)

    back_out[me] = partial[mine]

    @pl.loop(1, devices)
    def _(i):
        sta_copy(peer(i), me).wait_send()
        foot_copy(peer(i), me).wait_send()
        back_copy(peer(i), me).wait_send()
        back_copy(me, peer(i)).wait_recv()


def ranks(one_hot):
    size = one_hot.shape[0]
    at = jnp.arange(size, dtype=jnp.int32)
    lower = (at[:, None] > at[None, :]).astype(BF16)
    before = jnp.dot(lower, one_hot.astype(BF16), preferred_element_type=F32)
    return jnp.sum(before * one_hot, axis=1)


def exact_dot(left, right):
    return jnp.dot(left, right, precision=lax.Precision.HIGHEST, preferred_element_type=F32)


def shards(
    lon_count,
    lat_count,
    eta_adj,
    east_adj,
    north_adj,
    depth,
    station_owner,
    station_cell,
    station_misfit,
    footprints,
    foot_tile,
    foot_block,
    foot_source,
):
    devices = lon_count * lat_count
    rows, cols = eta_adj.shape
    records = station_cell.shape[0]
    feet = footprints.shape[0]
    capacity = max(2, 2 * records // devices)
    width = max(LANES, 2 * capacity)
    limit = max(8, 2 * feet // devices)
    slots = devices * limit
    group = slots // LANES
    me = lax.axis_index("lon") * lat_count + lax.axis_index("lat")
    names = jnp.arange(devices, dtype=jnp.int32)

    owner_hot = (station_owner == names[None, :]).astype(F32)
    rank = ranks(owner_hot)
    lanes = (jnp.arange(width, dtype=jnp.int32) % (width // 2)).astype(F32)
    slot_hot = (rank[:, None] == lanes[None, :]).astype(F32)
    period = jnp.arange(records, dtype=jnp.int32) // STA_DEV
    at_row = (period * rows + station_cell // cols).astype(F32)
    at_col = (station_cell % cols).astype(F32)
    spread = jnp.concatenate(
        [slot_hot * v[:, None] for v in (station_misfit, at_row, at_col)], axis=1
    )
    stations = exact_dot(owner_hot.T, spread).reshape(devices, 3, width)

    tile_hot = (foot_tile == names[None, :]).astype(F32)
    foot_place = foot_tile[:, 0] * limit + ranks(tile_hot).astype(jnp.int32)
    place_hot = (jnp.arange(slots, dtype=jnp.int32)[:, None] == foot_place[None, :]).astype(F32)
    foot_buffer = exact_dot(place_hot, footprints)
    ids = jnp.sum(place_hot * foot_block.astype(F32)[None, :], axis=1).reshape(devices, 1, limit)
    mine = (names == me).astype(F32)
    ids = (ids * mine[None, :, None]).reshape(devices, group, LANES)
    if width > LANES:
        ids = jnp.pad(ids, ((0, 0), (0, 0), (0, width - LANES)))
    packet = jnp.concatenate([stations, jnp.zeros((devices, 1, width), F32), ids], axis=1)
    depth_of = packet.shape[1]
    packet = jnp.pad(packet, ((0, 0), (0, -depth_of % 8), (0, 0)))
    depth_of = packet.shape[1]

    source_hot = (foot_source[:, None] == jnp.arange(SRC_DEV, dtype=jnp.int32)[None, :]).astype(F32)
    source_of = exact_dot(place_hot, source_hot)

    tall, wide = rows + 2 * EDGE, cols + LANES
    count = (rows // BH) * (cols // BW)
    vmem = pl.BlockSpec(memory_space=pltpu.VMEM)
    field = jax.ShapeDtypeStruct((rows, cols), F32)
    eta, east, north, back = pl.pallas_call(
        functools.partial(kernel, lon_count, lat_count, limit),
        out_shape=(field, field, field, jax.ShapeDtypeStruct((devices, 8, LANES), F32)),
        in_specs=[vmem] * 6,
        out_specs=(vmem,) * 4,
        scratch_shapes=[
            pltpu.VMEM((devices, depth_of, width), F32),
            pltpu.VMEM((slots, BH * BW), F32),
            pltpu.VMEM((FIELDS, tall, wide), F32),
            pltpu.VMEM((rows, LANES), F32),
            pltpu.VMEM((rows, LANES), F32),
            pltpu.VMEM((rows, LANES), F32),
            pltpu.VMEM((rows, LANES), F32),
            pltpu.VMEM((ITERS * count, BH * BW), F32),
            pltpu.VMEM((group, 8, LANES), F32),
            pltpu.VMEM((group, 8, LANES), F32),
            pltpu.SemaphoreType.DMA((devices,)),
            pltpu.SemaphoreType.DMA((devices,)),
            pltpu.SemaphoreType.DMA((devices,)),
            pltpu.SemaphoreType.DMA((devices,)),
            pltpu.SemaphoreType.DMA((devices,)),
            pltpu.SemaphoreType.DMA((devices,)),
            pltpu.SemaphoreType.DMA((4,)),
            pltpu.SemaphoreType.DMA((4,)),
        ],
        compiler_params=pltpu.CompilerParams(
            collective_id=0, has_side_effects=True, vmem_limit_bytes=60 * 1024 * 1024
        ),
    )(eta_adj, east_adj, north_adj, depth, packet, foot_buffer)

    start = lax.rem(me, devices // group) * limit
    mine_back = lax.dynamic_slice(back, (0, 0, start), (devices, ITERS, limit))
    by_slot = mine_back.transpose(1, 0, 2).reshape(ITERS, slots)
    uplift_grad = exact_dot(by_slot, source_of)
    return eta, east, north, uplift_grad


def solution(mesh):
    in_specs = (
        P("lat", "lon"),
        P("lat", "lon"),
        P("lat", "lon"),
        P("lat", "lon"),
        P(("lon", "lat"), None),
        P(("lon", "lat")),
        P(("lon", "lat")),
        P(("lon", "lat"), None),
        P(("lon", "lat"), None),
        P(("lon", "lat")),
        P(("lon", "lat")),
    )
    out_specs = (P("lat", "lon"), P("lat", "lon"), P("lat", "lon"), P(None, ("lon", "lat")))
    body = functools.partial(shards, mesh.shape["lon"], mesh.shape["lat"])
    return jax.shard_map(body, mesh=mesh, in_specs=in_specs, out_specs=out_specs, check_vma=False)
```
